32 devices in a mesh: row: 8 (over y, x, core), col: 4 (over z).
Axes of the slice: x: 2, y: 2, z: 4, core: 2. Of those that a mesh axis runs over, the one named last changes fastest.
Arguments:
- hidden_in: bfloat16 [8192, 2560], P('row', 'col')
- cotangent: bfloat16 [8192, 2560], P('row', 'col')
- lengths: int32 [8], P('row'), may hold values from 512 to 1024, as said below
- piece_starts: int32 [8, 2], P('row'), may hold values from 0 to 768, as said below
- norm_in: bfloat16 [2560], P('row'), may hold values from 0.25 to 1.75
- wq_down: bfloat16 [2560, 768], P('row', 'col'), may hold values from -0.125 to 0.125
- q_norm: bfloat16 [768], P('row'), may hold values from 0.25 to 1.75
- wq_up: bfloat16 [768, 3840], P('row', 'col'), may hold values from -0.3125 to 0.3125
- wkv_down: bfloat16 [2560, 288], P('row', 'col'), may hold values from -0.125 to 0.125
- kv_norm: bfloat16 [256], P('row'), may hold values from 0.25 to 1.75
- wkv_up: bfloat16 [256, 5120], P('row', 'col'), may hold values from -0.375 to 0.375
- w_out: bfloat16 [2560, 2560], P('col', 'row'), may hold values from -2 to 2
- norm_mid: bfloat16 [2560], P('row'), may hold values from 0.25 to 1.75
- w_gate: bfloat16 [2560, 6400], P('row', 'col'), may hold values from -0.125 to 0.125
- w_up: bfloat16 [2560, 6400], P('row', 'col'), may hold values from -0.125 to 0.125
- w_down: bfloat16 [6400, 2560], P('col', 'row'), may hold values from -0.3125 to 0.3125
Outputs:
- layer_out: bfloat16 [8192, 2560], P('row', 'col')
- input_grad: bfloat16 [8192, 2560], P('row', 'col')
- grad_norm_in: float32 [2560], P('row')
- grad_wq_down: float32 [2560, 768], P('row', 'col')
- grad_q_norm: float32 [768], P('row')
- grad_wq_up: float32 [768, 3840], P('row', 'col')
- grad_wkv_down: float32 [2560, 288], P('row', 'col')
- grad_kv_norm: float32 [256], P('row')
- grad_wkv_up: float32 [256, 5120], P('row', 'col')
- grad_w_out: float32 [2560, 2560], P('col', 'row')
- grad_norm_mid: float32 [2560], P('row')
- grad_w_gate: float32 [2560, 6400], P('row', 'col')
- grad_w_up: float32 [2560, 6400], P('row', 'col')
- grad_w_down: float32 [6400, 2560], P('col', 'row')
- statistics: float32 [5], replicated
The draws below stay inside these ranges and needn't reach their ends.
Inputs may be any that keep to these rules, and one draw needn't show every extreme that they name: `lengths`: the valid tokens of a sequence are its first ones; some sequence is full and some holds half of 1024. `piece_starts`: piece k of a sequence starts between k * 2 * 256 and (2 * k + 1) * 256, so pieces are disjoint, ascending and inside the sequence.
All inputs are finite; a program needn't handle non-finite values.
Results may differ from the reference program's by a relative error of at most 0.025.
Values may be sent and summed in bfloat16 or wider, within the bound.
No kernel may reach another device: no remote copies, remote signals or barrier semaphores. Data moves between devices by JAX's collectives and lax.ppermute only.
A program may use at most 256 MiB of HBM per device.

```python
import math
import jax
import jax.numpy as jnp
from jax import lax

D = 2560
QR = 768
KVR = 256
H = 40
NOPE = 64
ROPE = 32
V = 64
FF = 6400
PIECE = 256
SEQ_LEN = 1024
SEQS = 8
TOKENS = 8192
PIECES = 2


def token_ramp():
    return (jnp.arange(TOKENS).astype(jnp.float32) / TOKENS)[:, None]


def draw_hidden_in(key, part):
    inner = jax.random.fold_in(key, 3)
    ramp = token_ramp()
    base = jnp.clip(jax.random.normal(inner, (TOKENS, D), jnp.float32), -6.0, 6.0)
    level = 0.25 * (1.0 + 2.0 * ramp)
    return (base * level).astype(jnp.bfloat16)


def draw_cotangent(key, part):
    inner = jax.random.fold_in(key, 11)
    ramp = token_ramp()
    base = jnp.clip(jax.random.normal(inner, (TOKENS, D), jnp.float32), -6.0, 6.0)
    level = 1.0 + 2.0 * ramp
    return (base * level).astype(jnp.bfloat16)


def draw_lengths(key, part):
    inner = jax.random.fold_in(key, 5)
    drawn = jax.random.randint(inner, (SEQS,), SEQ_LEN // 2, SEQ_LEN + 1, dtype=jnp.int32)
    chosen = jax.random.randint(jax.random.fold_in(inner, 1), (), 0, SEQS, dtype=jnp.int32)
    places = jnp.arange(SEQS, dtype=jnp.int32)
    drawn = jnp.where(places == chosen, SEQ_LEN, drawn)
    drawn = jnp.where(places == (chosen + 1) % SEQS, SEQ_LEN // 2, drawn)
    return drawn.astype(jnp.int32)


def draw_piece_starts(key, part):
    inner = jax.random.fold_in(key, 9)
    shifts = jax.random.randint(inner, (SEQS, PIECES), 0, PIECE + 1, dtype=jnp.int32)
    chosen = jax.random.randint(jax.random.fold_in(inner, 1), (), 0, SEQS, dtype=jnp.int32)
    seq_ids = jnp.arange(SEQS, dtype=jnp.int32)[:, None]
    piece_ids = jnp.arange(PIECES, dtype=jnp.int32)[None, :]
    shifts = jnp.where((seq_ids == chosen) & (piece_ids == PIECES - 1), PIECE, shifts)
    shifts = jnp.where((seq_ids == (chosen + 1) % SEQS) & (piece_ids == 0), 0, shifts)
    return (piece_ids * 2 * PIECE + shifts).astype(jnp.int32)


def steps_of(rng, extent, cuts, smallest, high):
    level, own = 1.0, jax.random.fold_in(rng, 6)
    for axis_at, blocks in cuts:
        steps = jnp.exp(jax.random.uniform(jax.random.fold_in(own, axis_at), (blocks,), jnp.float32, smallest / len(cuts), high / len(cuts)))
        level = level * jnp.repeat(steps, extent[axis_at] // blocks).reshape([-1 if axis == axis_at else 1 for axis in range(len(extent))])
    return level


def bell_draw(rng, dims, scale, reach, cuts=(), kind=jnp.bfloat16):
    factor_of = steps_of(rng, dims, cuts, -0.22, 0.18) if cuts else 1.0
    values = jax.random.normal(rng, dims, jnp.float32) * scale * factor_of
    return jnp.minimum(jnp.maximum(values, -reach), reach).astype(kind)


def setup_inputs(seed: int = 0) -> dict:
    key_list = jax.random.split(jax.random.key(seed), 17)
    hidden_in = draw_hidden_in(jax.random.fold_in(key_list[16], 71), 0)
    cotangent = draw_cotangent(jax.random.fold_in(key_list[16], 71), 0)
    lengths = draw_lengths(jax.random.fold_in(key_list[16], 71), 0)
    piece_starts = draw_piece_starts(jax.random.fold_in(key_list[16], 71), 0)
    norm_in = jnp.clip(1.0 + 0.15 * jax.random.normal(key_list[4], (D,), jnp.float32), 0.25, 1.75).astype(jnp.bfloat16)
    wq_down = bell_draw(key_list[5], (D, QR), D ** -0.5, 0.125, ((0, 8), (1, 4)))
    q_norm = jnp.clip(1.0 + 0.15 * jax.random.normal(key_list[6], (QR,), jnp.float32), 0.25, 1.75).astype(jnp.bfloat16)
    wq_up = bell_draw(key_list[7], (QR, H * (NOPE + ROPE)), (QR // 2) ** -0.5, 0.3125, ((0, 8), (1, 4)))
    wkv_down = bell_draw(key_list[8], (D, KVR + ROPE), D ** -0.5, 0.125, ((0, 8), (1, 4)))
    kv_norm = jnp.clip(1.0 + 0.15 * jax.random.normal(key_list[9], (KVR,), jnp.float32), 0.25, 1.75).astype(jnp.bfloat16)
    wkv_up = bell_draw(key_list[10], (KVR, H * (NOPE + V)), KVR ** -0.5, 0.375, ((0, 8), (1, 4)))
    w_out = bell_draw(key_list[11], (H * V, D), (max(H * V // 256, 4)) ** -0.5, 2.0, ((0, 4), (1, 8)))
    norm_mid = jnp.clip(1.0 + 0.15 * jax.random.normal(key_list[12], (D,), jnp.float32), 0.25, 1.75).astype(jnp.bfloat16)
    w_gate = bell_draw(key_list[13], (D, FF), D ** -0.5, 0.125, ((0, 8), (1, 4)))
    w_up = bell_draw(key_list[14], (D, FF), D ** -0.5, 0.125, ((0, 8), (1, 4)))
    w_down = bell_draw(key_list[15], (FF, D), (FF // 16) ** -0.5, 0.3125, ((0, 4), (1, 8)))
    return dict(hidden_in=hidden_in, cotangent=cotangent, lengths=lengths, piece_starts=piece_starts, norm_in=norm_in, wq_down=wq_down, q_norm=q_norm, wq_up=wq_up, wkv_down=wkv_down, kv_norm=kv_norm, wkv_up=wkv_up, w_out=w_out, norm_mid=norm_mid, w_gate=w_gate, w_up=w_up, w_down=w_down)


@jax.custom_vjp
def low(v):
    return lax.optimization_barrier(v.astype(jnp.bfloat16)).astype(jnp.float32)

@jax.custom_vjp
def low_back(v):
    return v

def low_keep(v):
    return (low(v), None)

def low_pass(kept, grad):
    return (grad,)

def back_keep(v):
    return (v, None)

def back_low(kept, grad):
    return (low(grad),)
low.defvjp(low_keep, low_pass)
low_back.defvjp(back_keep, back_low)
epsilon = 1e-05
branch_scale = 1.4 / math.sqrt(62.0)
masked_score = -1000000000.0
highest = lax.Precision.HIGHEST

def matmul(left, right):
    return jnp.dot(left, right, precision=highest)

def rms_norm(values):
    return values * lax.rsqrt(lax.optimization_barrier(jnp.mean(values * values, axis=-1, keepdims=True)) + epsilon)

def rotary_tables(count):
    places = (jnp.arange(count).astype(jnp.int32) % SEQ_LEN).astype(jnp.float32)
    half = ROPE // 2
    freqs = 10000.0 ** (-(jnp.arange(half).astype(jnp.float32) * 2.0 / ROPE))
    angles = places[:, None] * freqs[None, :]
    return (jnp.cos(angles), jnp.sin(angles))

def rotate(values, cosine, sine):
    half = values.shape[-1] // 2
    first = values[..., :half]
    second = values[..., half:]
    return jnp.concatenate([first * cosine - second * sine, second * cosine + first * sine], axis=-1)

def piece_index(places, starts):
    hits = (places[:, None] >= starts[None, :]) & (places[:, None] < starts[None, :] + PIECE)
    labels = (jnp.arange(PIECES) + 1).astype(jnp.int32)
    return lax.optimization_barrier(jnp.sum(jnp.where(hits, labels[None, :], 0), axis=1)).astype(jnp.int32) - 1

def visible(length, starts):
    places = jnp.arange(SEQ_LEN).astype(jnp.int32)
    pieces = piece_index(places, starts)
    causal = places[None, :] <= places[:, None]
    shared = (pieces[:, None] == pieces[None, :]) & (pieces[:, None] >= 0)
    return (places[None, :] < length) & (causal | shared)

def attend(items):
    q_nope, q_rope, k_nope, k_rope, values, length, starts = items
    scale = 1.0 / math.sqrt(NOPE + ROPE)
    allowed = visible(length, starts)
    scores = jnp.einsum('qhd,khd->hqk', q_nope, k_nope, precision=highest)
    scores = scores + jnp.einsum('qhd,kd->hqk', q_rope, k_rope, precision=highest)
    scores = jnp.where(allowed[None], scores * scale, masked_score)
    scores = low_back(scores)
    prob = low(jax.nn.softmax(scores, axis=-1))
    outputs = jnp.einsum('hqk,khd->qhd', prob, values, precision=highest)
    return low_back(low(outputs))

def reference(hidden_in, cotangent, lengths, piece_starts, norm_in, wq_down, q_norm, wq_up, wkv_down, kv_norm, wkv_up, w_out, norm_mid, w_gate, w_up, w_down):
    cosine, sine = rotary_tables(TOKENS)

    def forward(x_in, gain_in, wqa, gain_q, wqb, wkva, gain_kv, wkvb, wout, gain_mid, wgate, wupper, wdown):
        normed_in = low(rms_norm(x_in) * gain_in)
        q_latent = low_back(low(matmul(normed_in, wqa)))
        kv_latent = low_back(low(matmul(normed_in, wkva)))
        q_normed = low(rms_norm(q_latent) * gain_q)
        kv_normed = low(rms_norm(kv_latent[:, :KVR]) * gain_kv)
        k_rope = low(rotate(kv_latent[:, KVR:], cosine, sine))
        q_raw = low_back(matmul(q_normed, wqb)).reshape(TOKENS, H, NOPE + ROPE)
        q_nope = low(q_raw[:, :, :NOPE])
        q_rope = low(rotate(q_raw[:, :, NOPE:], cosine[:, None, :], sine[:, None, :]))
        kv_raw = low_back(matmul(kv_normed, wkvb)).reshape(TOKENS, H, NOPE + V)
        k_nope = low(kv_raw[:, :, :NOPE])
        values = low(kv_raw[:, :, NOPE:])
        stacked = (q_nope.reshape(SEQS, SEQ_LEN, H, NOPE), q_rope.reshape(SEQS, SEQ_LEN, H, ROPE), k_nope.reshape(SEQS, SEQ_LEN, H, NOPE), k_rope.reshape(SEQS, SEQ_LEN, ROPE), values.reshape(SEQS, SEQ_LEN, H, V), lengths, piece_starts)
        heads_out = lax.map(jax.checkpoint(attend), stacked)
        attended = heads_out.reshape(TOKENS, H * V)
        attn = low_back(matmul(attended, wout))
        mid = x_in + branch_scale * attn
        normed_mid = low(rms_norm(mid) * gain_mid)
        gate = low_back(matmul(normed_mid, wgate))
        upper = low_back(matmul(normed_mid, wupper))
        act = low(jax.nn.silu(gate) * upper)
        mlp = low_back(matmul(act, wdown))
        result = mid + branch_scale * mlp
        return (result, (attn, mlp, act))
    floats = [v.astype(jnp.float32) for v in (hidden_in, norm_in, wq_down, q_norm, wq_up, wkv_down, kv_norm, wkv_up, w_out, norm_mid, w_gate, w_up, w_down)]
    result, pullback, extras = jax.vjp(forward, *floats, has_aux=True)
    grads = pullback(cotangent.astype(jnp.float32))
    attn, mlp, act = extras
    d_input = grads[0]
    valid = (jnp.arange(SEQ_LEN).astype(jnp.int32)[None, :] < lengths[:, None]).reshape(TOKENS).astype(jnp.float32)[:, None]
    total_valid = jnp.sum(lengths).astype(jnp.float32)
    pieces = [branch_scale * attn, branch_scale * mlp, result, act, d_input]
    widths = [D, D, D, FF, D]
    statistics = jnp.stack([jnp.sqrt(jnp.sum(valid * p * p) / (total_valid * w)) for p, w in zip(pieces, widths)])
    return (result.astype(jnp.bfloat16), d_input.astype(jnp.bfloat16), grads[1], grads[2], grads[3], grads[4], grads[5], grads[6], grads[7], grads[8], grads[9], grads[10], grads[11], grads[12], statistics)
```

```python
import functools
import math

import jax
import jax.numpy as jnp
from jax import lax
from jax.experimental import pallas as pl
from jax.experimental.pallas import tpu as pltpu
from jax.sharding import PartitionSpec as P

NOPE = 64
ROPE = 32
V = 64
PIECE = 256
LANES = 128
ROWS = 256

epsilon = 1e-05
branch_scale = 1.4 / math.sqrt(62.0)
masked_score = -1000000000.0
score_scale = 1.0 / math.sqrt(NOPE + ROPE)
log2e = math.log2(math.e)

f32 = jnp.float32
bf16 = jnp.bfloat16


def matmul(left, right):
    return jnp.dot(left, right, preferred_element_type=f32)


def matmul_nt(left, right):
    return lax.dot_general(left, right, (((1,), (1,)), ((), ())), preferred_element_type=f32)


def matmul_tn(left, right):
    return lax.dot_general(left, right, (((0,), (0,)), ((), ())), preferred_element_type=f32)


def inverse_rms(values):
    return lax.rsqrt(jnp.mean(values * values, axis=1, keepdims=True) + epsilon)


def norm_back(grad_in, values, inverse, gain):
    scaled = grad_in * gain
    return inverse * scaled - values * inverse**3 * jnp.mean(scaled * values, axis=1, keepdims=True)


def rotary_tables(places):
    half = ROPE // 2
    freqs = 10000.0 ** (-(jnp.arange(half).astype(f32) * 2.0 / ROPE))
    angles = places.astype(f32)[:, None] * freqs[None, :]
    return (jnp.cos(angles), jnp.sin(angles))


def rotate(values, cosine, sine):
    half = values.shape[-1] // 2
    first = values[..., :half]
    second = values[..., half:]
    return jnp.concatenate(
        [first * cosine - second * sine, second * cosine + first * sine], axis=-1
    )


NEAR = ((0, 1), (1, 0), (2, 3), (3, 2))
MIDDLE = ((1, 2), (2, 1))
OUTWARD = ((1, 0), (2, 3))
INWARD = ((0, 1), (3, 2))


def after(value, *others):
    return lax.optimization_barrier((value,) + others)[0]


def slot_ids(me, n):
    if n != 4:
        return [lax.rem(me + j, n) for j in range(n)]
    end = (me == 0) | (me == 3)
    return [me, me ^ 1, jnp.where(end, me ^ 2, me ^ 3), jnp.where(end, me ^ 3, me ^ 2)]


def spread(value, me, n):
    if n != 4:
        whole = lax.all_gather(value, "col", axis=0)
        return [lax.dynamic_index_in_dim(whole, at, 0, False) for at in slot_ids(me, n)]
    near = lax.ppermute(value, "col", NEAR)
    across = lax.ppermute(value, "col", MIDDLE)
    second = lax.ppermute(across, "col", OUTWARD)
    third = lax.ppermute(near, "col", MIDDLE)
    last = lax.ppermute(third, "col", OUTWARD)
    end = (me == 0) | (me == 3)
    return [value, near, jnp.where(end, second, across), jnp.where(end, last, third)]


def place(slots, ids, axis=0):
    size = slots[0].shape[axis]
    shape = list(slots[0].shape)
    shape[axis] = size * len(slots)
    whole = jnp.zeros(shape, slots[0].dtype)
    for block, at in zip(slots, ids):
        whole = lax.dynamic_update_slice_in_dim(whole, block, at * size, axis)
    return whole


def collect(parts, ids, me, n):
    if n != 4:
        blocks = [part().astype(bf16) for part in parts]
        return lax.psum_scatter(
            place(blocks, ids), "col", scatter_dimension=0, tiled=True
        ).astype(f32)
    q3 = lax.optimization_barrier(parts[3]().astype(bf16))
    first = lax.ppermute(q3, "col", INWARD)
    q2 = lax.optimization_barrier(parts[2]().astype(bf16))
    q1 = lax.optimization_barrier(parts[1]().astype(bf16))
    q0 = parts[0]()
    third = lax.ppermute((q3.astype(f32) + first.astype(f32)).astype(bf16), "col", MIDDLE)
    second = lax.ppermute(after(q2, first), "col", INWARD)
    near = lax.ppermute((q1.astype(f32) + third.astype(f32)).astype(bf16), "col", NEAR)
    across = lax.ppermute((q2.astype(f32) + second.astype(f32)).astype(bf16), "col", MIDDLE)
    return q0 + near.astype(f32) + across.astype(f32)


NN = (((1,), (0,)), ((), ()))
NT = (((1,), (1,)), ((), ()))


def dot(left, right, dims):
    return lax.dot_general(left, right, dims, preferred_element_type=f32)


def lane_ids(rows):
    return lax.broadcasted_iota(jnp.int32, (rows, LANES), 1)


def fill_bias(scalars, chunk, count, pieces, bias_ref):
    shape = (count, ROWS)
    keys = lax.broadcasted_iota(jnp.int32, shape, 0)
    queries = lax.broadcasted_iota(jnp.int32, shape, 1) + chunk * ROWS
    seen = keys <= queries
    for piece in range(pieces):
        start = scalars[1 + piece]
        both = (jnp.minimum(keys, queries) >= start) & (jnp.maximum(keys, queries) < start + PIECE)
        seen = seen | both
    seen = seen & (keys < scalars[0])
    bias_ref[chunk] = jnp.where(seen, 0.0, masked_score)


def key_blocks(scalars, chunk, count, pieces):
    last = chunk * ROWS + (ROWS - 1)
    reach = last
    for piece in range(pieces):
        start = scalars[1 + piece]
        inside = (start <= last) & (last < start + PIECE)
        reach = jnp.maximum(reach, jnp.where(inside, start + PIECE - 1, 0))
    reach = jnp.minimum(reach, scalars[0] - 1)
    return reach // ROWS + 1


def turn(values, cosine, sine_up, sine_down):
    half = ROPE // 2
    return (
        values * cosine
        + pltpu.roll(values, LANES - half, 1) * sine_up
        + pltpu.roll(values, half, 1) * sine_down
    )


def forward_kernel(
    count, pieces, scalars, q_ref, kv_ref, kp_ref, cos_ref, up_ref, down_ref,
    o_ref, rot_ref, log_ref, bias_ref, key_ref, value_ref,
):
    pair, chunk = pl.program_id(0), pl.program_id(1)
    low = lane_ids(count) < NOPE

    @pl.when(pair == 0)
    def _():
        fill_bias(scalars, chunk, count, pieces, bias_ref)

    @pl.when(chunk == 0)
    def _():
        for head in range(2):
            kv = kv_ref[:, head * LANES : (head + 1) * LANES].astype(f32)
            key_ref[head] = jnp.where(low, kv, kp_ref[...].astype(f32)).astype(bf16)
            value_ref[head] = kv.T[NOPE:, :].astype(bf16)

    cosine, sine_up, sine_down = cos_ref[...], up_ref[...], down_ref[...]
    for head in range(2):
        at = slice(head * LANES, (head + 1) * LANES)
        rot_ref[:, at] = turn(q_ref[:, at], cosine, sine_up, sine_down).astype(bf16)
    blocks = key_blocks(scalars, chunk, count, pieces)

    def run(size):
        halves = []
        for head in range(2):
            query = rot_ref[:, head * LANES : (head + 1) * LANES]
            scores = dot(key_ref[head, :size, :], query, NT)
            scores = scores * (score_scale * log2e) + bias_ref[chunk, :size, :]
            largest = jnp.max(scores, axis=0, keepdims=True)
            expos = jnp.exp2(scores - largest)
            total = jnp.sum(expos, axis=0, keepdims=True)
            log_ref[head : head + 1, :] = largest + jnp.log2(total)
            out = dot(value_ref[head, :, :size], expos.astype(bf16), NN)
            halves.append(out / total)
        o_ref[...] = jnp.concatenate(halves, axis=0).T.astype(bf16)

    for number in range(1, count // ROWS + 1):
        pl.when(blocks == number)(functools.partial(run, number * ROWS))


def backward_kernel(
    count, pieces, scalars, q_ref, kv_ref, kp_ref, cos_ref, up_ref, down_ref, do_ref, log_ref,
    gq_ref, gkv_ref, dkp_ref, bias_ref, key_ref, turned_ref, value_ref, dk_ref, dv_ref,
):
    pair, chunk = pl.program_id(0), pl.program_id(1)
    lanes = lane_ids(count)
    low = lanes < NOPE

    @pl.when(pair == 0)
    def _():
        fill_bias(scalars, chunk, count, pieces, bias_ref)

    @pl.when((pair == 0) & (chunk == 0))
    def _():
        dkp_ref[...] = jnp.zeros_like(dkp_ref)

    @pl.when(chunk == 0)
    def _():
        for head in range(2):
            kv = kv_ref[:, head * LANES : (head + 1) * LANES].astype(f32)
            key = jnp.where(low, kv, kp_ref[...].astype(f32))
            key_ref[head] = key.astype(bf16)
            turned_ref[head] = key.T.astype(bf16)
            if head == 0:
                value_ref[head] = jnp.where(low, pltpu.roll(kv, NOPE, 1), 0.0).astype(bf16)
            else:
                value_ref[head] = jnp.where(low, 0.0, kv).astype(bf16)
        dk_ref[...] = jnp.zeros_like(dk_ref)
        dv_ref[...] = jnp.zeros_like(dv_ref)

    blocks = key_blocks(scalars, chunk, count, pieces)

    def run(size):
        d_out = do_ref[...]
        for head in range(2):
            at = slice(head * LANES, (head + 1) * LANES)
            query = q_ref[:, at]
            scores = dot(key_ref[head, :size, :], query, NT)
            scores = scores * (score_scale * log2e) + bias_ref[chunk, :size, :]
            prob = jnp.exp2(scores - log_ref[head : head + 1, :])
            d_prob = dot(value_ref[head, :size, :], d_out, NT)
            inner = jnp.sum(prob * d_prob, axis=0, keepdims=True)
            d_scores = (prob * (d_prob - inner)).astype(bf16)
            dv_ref[head, :size, :] += dot(prob.astype(bf16), d_out, NN)
            dk_ref[head, :size, :] += dot(d_scores, query, NN)
            d_query = dot(turned_ref[head, :, :size], d_scores, NN).T * score_scale
            gq_ref[:, at] = turn(d_query, cos_ref[...], -up_ref[...], -down_ref[...]).astype(bf16)

    for number in range(1, count // ROWS + 1):
        pl.when(blocks == number)(functools.partial(run, number * ROWS))

    @pl.when(chunk == pl.num_programs(1) - 1)
    def _():
        for head in range(2):
            at = slice(head * LANES, (head + 1) * LANES)
            d_key = dk_ref[head] * score_scale
            d_value = dv_ref[head]
            if head == 0:
                d_value = pltpu.roll(d_value, NOPE, 1)
            gkv_ref[:, at] = jnp.where(low, d_key, d_value).astype(bf16)
            dkp_ref[...] += jnp.where(low | (lanes >= NOPE + ROPE), 0.0, d_key)


def attention_specs(count):
    chunk = lambda width: pl.BlockSpec((ROWS, width), lambda p, c: (c, 0))
    by_pair = lambda width: pl.BlockSpec((ROWS, width), lambda p, c: (c, p))
    return dict(
        scalars=pl.BlockSpec(memory_space=pltpu.SMEM),
        q=by_pair(2 * LANES),
        kv=pl.BlockSpec((count, 2 * LANES), lambda p, c: (0, p)),
        kp=pl.BlockSpec((count, LANES), lambda p, c: (0, 0)),
        table=chunk(LANES),
        half=by_pair(LANES),
        log=pl.BlockSpec((8, ROWS), lambda p, c: (p, c)),
    )


def attention_forward(scalars, q_raw, kv, k_rope, tables):
    count = q_raw.shape[0]
    pairs = q_raw.shape[1] // (2 * LANES)
    pieces = scalars.shape[0] - 1
    chunks = count // ROWS
    s = attention_specs(count)
    return pl.pallas_call(
        functools.partial(forward_kernel, count, pieces),
        grid=(pairs, chunks),
        in_specs=[s["scalars"], s["q"], s["kv"], s["kp"], s["table"], s["table"], s["table"]],
        out_specs=[s["half"], s["q"], s["log"]],
        out_shape=[
            jax.ShapeDtypeStruct((count, pairs * LANES), bf16),
            jax.ShapeDtypeStruct((count, 2 * pairs * LANES), bf16),
            jax.ShapeDtypeStruct((8 * pairs, count), f32),
        ],
        scratch_shapes=[
            pltpu.VMEM((chunks, count, ROWS), f32),
            pltpu.VMEM((2, count, LANES), bf16),
            pltpu.VMEM((2, V, count), bf16),
        ],
        compiler_params=pltpu.CompilerParams(dimension_semantics=("arbitrary", "arbitrary")),
        name="attention_forward",
    )(scalars, q_raw, kv, k_rope, *tables)


def attention_backward(scalars, q, kv, k_rope, tables, d_out, logs):
    count = q.shape[0]
    pairs = q.shape[1] // (2 * LANES)
    pieces = scalars.shape[0] - 1
    chunks = count // ROWS
    s = attention_specs(count)
    return pl.pallas_call(
        functools.partial(backward_kernel, count, pieces),
        grid=(pairs, chunks),
        in_specs=[
            s["scalars"], s["q"], s["kv"], s["kp"], s["table"], s["table"], s["table"],
            s["half"], s["log"],
        ],
        out_specs=[s["q"], s["kv"], s["kp"]],
        out_shape=[
            jax.ShapeDtypeStruct((count, 2 * pairs * LANES), bf16),
            jax.ShapeDtypeStruct((count, 2 * pairs * LANES), bf16),
            jax.ShapeDtypeStruct((count, LANES), f32),
        ],
        scratch_shapes=[
            pltpu.VMEM((chunks, count, ROWS), f32),
            pltpu.VMEM((2, count, LANES), bf16),
            pltpu.VMEM((2, LANES, count), bf16),
            pltpu.VMEM((2, count, LANES), bf16),
            pltpu.VMEM((2, count, LANES), f32),
            pltpu.VMEM((2, count, LANES), f32),
        ],
        compiler_params=pltpu.CompilerParams(dimension_semantics=("arbitrary", "arbitrary")),
        name="attention_backward",
    )(scalars, q, kv, k_rope, *tables, d_out, logs)


def visible(count, scalars):
    places = jnp.arange(count, dtype=jnp.int32)
    starts = scalars[1:]
    hits = (places[:, None] >= starts[None, :]) & (places[:, None] < starts[None, :] + PIECE)
    labels = jnp.arange(starts.shape[0], dtype=jnp.int32) + 1
    pieces = jnp.sum(jnp.where(hits, labels[None, :], 0), axis=1) - 1
    causal = places[None, :] <= places[:, None]
    shared = (pieces[:, None] == pieces[None, :]) & (pieces[:, None] >= 0)
    return (places[None, :] < scalars[0]) & (causal | shared)


def plain_turn(values, tables):
    half = ROPE // 2
    cosine, sine_up, sine_down = tables
    return (
        values * cosine[:, None, :]
        + jnp.roll(values, -half, 2) * sine_up[:, None, :]
        + jnp.roll(values, half, 2) * sine_down[:, None, :]
    )


def plain_keys(kv, k_rope, heads):
    count = kv.shape[0]
    kv = kv.reshape(count, heads, LANES)
    keys = jnp.where(jnp.arange(LANES) < NOPE, kv, k_rope[:, None, :])
    return keys, kv[:, :, NOPE:]


def plain_forward(scalars, q_raw, kv, k_rope, tables):
    count = q_raw.shape[0]
    heads = q_raw.shape[1] // LANES
    keys, values = plain_keys(kv, k_rope, heads)
    q = plain_turn(q_raw.reshape(count, heads, LANES), tables).astype(bf16)
    scores = jnp.einsum("qhd,khd->hqk", q, keys, preferred_element_type=f32) * score_scale
    scores = jnp.where(visible(count, scalars)[None], scores, masked_score)
    logs = jax.nn.logsumexp(scores, axis=2, keepdims=True)
    prob = jnp.exp(scores - logs).astype(bf16)
    out = jnp.einsum("hqk,khd->qhd", prob, values, preferred_element_type=f32).astype(bf16)
    return out.reshape(count, heads * V), q.reshape(count, heads * LANES), logs


def plain_backward(scalars, q, kv, k_rope, tables, d_out, logs):
    count = q.shape[0]
    heads = q.shape[1] // LANES
    keys, values = plain_keys(kv, k_rope, heads)
    q = q.reshape(count, heads, LANES)
    d_out = d_out.reshape(count, heads, V)
    scores = jnp.einsum("qhd,khd->hqk", q, keys, preferred_element_type=f32) * score_scale
    scores = jnp.where(visible(count, scalars)[None], scores, masked_score)
    prob = jnp.exp(scores - logs)
    d_prob = jnp.einsum("qhd,khd->hqk", d_out, values, preferred_element_type=f32)
    inner = jnp.sum(prob * d_prob, axis=2, keepdims=True)
    d_scores = (prob * (d_prob - inner)).astype(bf16)
    d_value = jnp.einsum("hqk,qhd->khd", prob.astype(bf16), d_out, preferred_element_type=f32)
    d_key = jnp.einsum("hqk,qhd->khd", d_scores, q, preferred_element_type=f32) * score_scale
    d_query = jnp.einsum("hqk,khd->qhd", d_scores, keys, preferred_element_type=f32) * score_scale
    cosine, sine_up, sine_down = tables
    g_q = plain_turn(d_query, (cosine, -sine_up, -sine_down)).astype(bf16)
    g_kv = jnp.concatenate([d_key[:, :, :NOPE], d_value], axis=2).astype(bf16)
    lanes = jnp.arange(LANES)
    d_kp = jnp.where((lanes >= NOPE) & (lanes < NOPE + ROPE), jnp.sum(d_key, axis=1), 0.0)
    return g_q.reshape(count, heads * LANES), g_kv.reshape(count, heads * LANES), d_kp


def per_device(
    hidden_in,
    cotangent,
    lengths,
    piece_starts,
    norm_in,
    wq_down,
    q_norm,
    wq_up,
    wkv_down,
    kv_norm,
    wkv_up,
    w_out,
    norm_mid,
    w_gate,
    w_up,
    w_down,
):
    n = lax.axis_size("col")
    me = lax.axis_index("col")
    row_count = lax.axis_size("row")
    row = lax.axis_index("row")
    ids = slot_ids(me, n)
    count, own_cols = hidden_in.shape
    width = own_cols * n
    tokens = count // n
    heads = wq_up.shape[1] // (NOPE + ROPE)
    scalars = jnp.concatenate([lengths, piece_starts[0]]).astype(jnp.int32)
    kernels = heads % 2 == 0 and count % ROWS == 0

    q_cols, kv_cols = wq_down.shape[1], wkv_down.shape[1]
    rank_q, rank_kv = q_cols * n, kv_cols * n - ROPE
    down_own = jnp.concatenate([wq_down, wkv_down], axis=1)
    down_all = lax.all_gather(down_own, "col", axis=0)
    down_all = jnp.concatenate(
        [down_all[j, :, :q_cols] for j in range(n)] + [down_all[j, :, q_cols:] for j in range(n)],
        axis=1,
    )
    gain_parts = jnp.concatenate([norm_in, q_norm, kv_norm, norm_mid])
    gains = lax.all_gather(gain_parts, "row", axis=0).astype(f32)
    edges = [0]
    for part in (norm_in, q_norm, kv_norm, norm_mid):
        edges.append(edges[-1] + part.shape[0])
    gain_in, gain_q, gain_kv, gain_mid = (
        gains[:, edges[j] : edges[j + 1]].reshape(-1) for j in range(4)
    )
    w_latent = lax.all_gather(down_all, "row", axis=0, tiled=True)
    pad = LANES - NOPE - ROPE
    wq_wide = jnp.pad(wq_up.reshape(-1, heads, NOPE + ROPE), ((0, 0), (0, 0), (0, pad)))
    wqb = lax.all_gather(wq_wide.reshape(-1, heads * LANES), "row", axis=0, tiled=True)
    wkvb = lax.all_gather(wkv_up, "row", axis=0, tiled=True)
    wout_t = lax.all_gather(w_out.T, "row", axis=0, tiled=True)
    wgate = lax.all_gather(w_gate, "row", axis=0, tiled=True)
    wupper = lax.all_gather(w_up, "row", axis=0, tiled=True)
    wdown_t = lax.all_gather(w_down.T, "row", axis=0, tiled=True)

    x_bf = lax.all_to_all(hidden_in, "col", split_axis=0, concat_axis=1, tiled=True)
    x = x_bf.astype(f32)
    inverse_in = inverse_rms(x)
    h1 = (x * inverse_in * gain_in).astype(bf16)
    latent = matmul(h1, w_latent).astype(bf16)
    q_lat = latent[:, :rank_q].astype(f32)
    kv_lat = latent[:, rank_q : rank_q + rank_kv].astype(f32)
    inverse_q = inverse_rms(q_lat)
    inverse_kv = inverse_rms(kv_lat)
    places = me * tokens + jnp.arange(tokens, dtype=jnp.int32)
    cosine, sine = rotary_tables(places)
    rope = rotate(latent[:, rank_q + rank_kv :].astype(f32), cosine, sine)
    normed = jnp.concatenate(
        [
            q_lat * inverse_q * gain_q,
            kv_lat * inverse_kv * gain_kv,
            jnp.zeros((tokens, NOPE), f32),
            rope,
            jnp.zeros((tokens, pad), f32),
        ],
        axis=1,
    ).astype(bf16)
    latents = place(spread(normed, me, n), ids)
    cot = place(spread(after(cotangent, x_bf), me, n), ids, 1)
    q_normed = latents[:, :rank_q]
    kv_normed = latents[:, rank_q : rank_q + rank_kv]
    k_rope = latents[:, rank_q + rank_kv :]

    q_raw = matmul(q_normed, wqb)
    kv = matmul(kv_normed, wkvb).astype(bf16)
    all_cos, all_sin = rotary_tables(jnp.arange(count, dtype=jnp.int32))
    ones, none = jnp.ones((count, NOPE), f32), jnp.zeros((count, NOPE), f32)
    tail, gap = jnp.zeros((count, pad), f32), jnp.zeros((count, ROPE // 2), f32)
    tables = (
        jnp.concatenate([ones, all_cos, all_cos, tail], axis=1),
        jnp.concatenate([none, -all_sin, gap, tail], axis=1),
        jnp.concatenate([none, gap, all_sin, tail], axis=1),
    )
    forward = attention_forward if kernels else plain_forward
    backward = attention_backward if kernels else plain_backward
    o, q_turned, logs = forward(scalars, q_raw, kv, k_rope, tables)

    def rows_of(array, at):
        return lax.dynamic_slice_in_dim(array, at * tokens, tokens, 0)

    attn = collect(
        [lambda at=at: matmul_nt(rows_of(o, at), wout_t) for at in ids], ids, me, n
    )
    mid = x + branch_scale * attn
    inverse_mid = inverse_rms(mid)
    h2 = (mid * inverse_mid * gain_mid).astype(bf16)

    h2_slots = spread(h2, me, n)
    g_mlp = (branch_scale * cot.astype(f32)).astype(bf16)
    valid = (jnp.arange(count, dtype=jnp.int32) < lengths[0]).astype(f32)[:, None]
    acts, g_gates, g_uppers = [], [], []
    act_square = 0.0
    for block, at in zip(h2_slots, ids):
        d_act = matmul(rows_of(g_mlp, at), wdown_t)
        gate = matmul(block, wgate)
        upper = matmul(block, wupper)
        sigma = jax.nn.sigmoid(gate)
        act = (gate * sigma * upper).astype(bf16)
        g_gates.append((d_act * upper * sigma * (1.0 + gate * (1.0 - sigma))).astype(bf16))
        g_uppers.append((d_act * gate * sigma).astype(bf16))
        acts.append(act)
        wide = act.astype(f32)
        act_square = act_square + jnp.sum(rows_of(valid, at) * wide * wide)
    d_h2 = collect(
        [
            lambda a=a, b=b: matmul_nt(a, wgate) + matmul_nt(b, wupper)
            for a, b in zip(g_gates, g_uppers)
        ],
        ids, me, n,
    )
    dy = rows_of(cot, me).astype(f32)
    d_mid = dy + norm_back(d_h2, mid, inverse_mid, gain_mid)
    grad_gain_mid = jnp.sum(d_h2 * mid * inverse_mid, axis=0)
    g_attn = place(spread((branch_scale * d_mid).astype(bf16), me, n), ids)

    h2_all = place(h2_slots, ids)
    act_all = place(acts, ids)
    gate_all = place(g_gates, ids)
    upper_all = place(g_uppers, ids)

    def scatter(value):
        return lax.psum_scatter(value.astype(bf16), "row", scatter_dimension=0, tiled=True)

    grad_down = scatter(matmul_tn(g_mlp, act_all)).T.astype(f32)
    grad_gate = scatter(matmul_tn(h2_all, gate_all)).astype(f32)
    grad_upper = scatter(matmul_tn(h2_all, upper_all)).astype(f32)

    d_o = matmul(g_attn, wout_t).astype(bf16)
    grad_wout = scatter(matmul_tn(g_attn, o)).T.astype(f32)
    g_q, g_kv, d_kp = backward(scalars, q_turned, kv, k_rope, tables, d_o, logs)

    mlp = collect(
        [lambda a=a: matmul_nt(a, wdown_t) for a in acts], ids, me, n
    )
    result = mid + branch_scale * mlp
    layer_out = lax.all_to_all(
        result.astype(bf16), "col", split_axis=1, concat_axis=0, tiled=True
    )

    d_latents = jnp.concatenate(
        [
            matmul_nt(g_q, wqb).astype(bf16),
            matmul_nt(g_kv, wkvb).astype(bf16),
            d_kp.astype(bf16),
        ],
        axis=1,
    )
    d_latent = collect(
        [lambda at=at: rows_of(d_latents, at).astype(f32) for at in ids], ids, me, n
    )
    grad_wqb = scatter(matmul_tn(q_normed, g_q)).astype(f32)
    grad_wqb = grad_wqb.reshape(-1, heads, LANES)[:, :, : NOPE + ROPE]
    grad_wqb = grad_wqb.reshape(-1, heads * (NOPE + ROPE))
    grad_wkvb = scatter(matmul_tn(kv_normed, g_kv)).astype(f32)

    d_ql = d_latent[:, :rank_q]
    d_kvl = d_latent[:, rank_q : rank_q + rank_kv]
    d_rope = d_latent[:, rank_q + rank_kv + NOPE : rank_q + rank_kv + NOPE + ROPE]
    grad_gain_q = jnp.sum(d_ql * q_lat * inverse_q, axis=0)
    grad_gain_kv = jnp.sum(d_kvl * kv_lat * inverse_kv, axis=0)
    g_qa = norm_back(d_ql, q_lat, inverse_q, gain_q)
    g_kva = jnp.concatenate(
        [norm_back(d_kvl, kv_lat, inverse_kv, gain_kv), rotate(d_rope, cosine, -sine)], axis=1
    )
    g_lat = jnp.concatenate([g_qa, g_kva], axis=1).astype(bf16)
    d_h1 = matmul_nt(g_lat, w_latent)
    dx = d_mid + norm_back(d_h1, x, inverse_in, gain_in)
    grad_gain_in = jnp.sum(d_h1 * x * inverse_in, axis=0)
    input_grad = lax.all_to_all(dx.astype(bf16), "col", split_axis=1, concat_axis=0, tiled=True)

    g_cols = jnp.concatenate(
        [
            part
            for j in range(n)
            for part in (
                g_lat[:, j * q_cols : (j + 1) * q_cols],
                g_lat[:, rank_q + j * kv_cols : rank_q + (j + 1) * kv_cols],
            )
        ],
        axis=1,
    )
    g_all = place(spread(g_cols, me, n), ids)
    inverse_all = place(spread(inverse_in.reshape(1, tokens), me, n), ids).reshape(count, 1)
    gain_own = lax.dynamic_slice_in_dim(gain_in, me * own_cols, own_cols, 0)
    h1_own = (hidden_in.astype(f32) * inverse_all * gain_own).astype(bf16)
    grad_lat = scatter(matmul_tn(h1_own, g_all))
    moves = [(r * n + c, c * row_count + r) for r in range(row_count) for c in range(n)]
    grad_lat = lax.ppermute(grad_lat, ("row", "col"), moves)
    grad_lat = lax.all_to_all(
        grad_lat, "col", split_axis=1, concat_axis=0, tiled=True
    ).astype(f32)

    own_valid = rows_of(valid, me)
    attn_term = branch_scale * attn
    mlp_term = branch_scale * mlp
    square = lambda term: jnp.sum(own_valid * term * term)
    sums = jnp.stack(
        [
            square(attn_term),
            square(mlp_term),
            square(result),
            act_square,
            square(dx),
            jnp.sum(own_valid),
        ]
    )
    vector = jnp.concatenate([grad_gain_in, grad_gain_q, grad_gain_kv, grad_gain_mid, sums])
    vector = lax.psum(vector, ("row", "col"))
    gain_grads, at = [], 0
    for part in (norm_in, q_norm, kv_norm, norm_mid):
        size = part.shape[0]
        gain_grads.append(lax.dynamic_slice_in_dim(vector, at + row * size, size, 0))
        at += size * row_count
    totals = vector[at:]
    hidden_width = w_gate.shape[1] * n
    widths = jnp.array([width, width, width, hidden_width, width], f32)
    statistics = jnp.sqrt(totals[:5] / (totals[5] * widths))
    return (
        layer_out,
        input_grad,
        gain_grads[0],
        grad_lat[:, :q_cols],
        gain_grads[1],
        grad_wqb,
        grad_lat[:, q_cols:],
        gain_grads[2],
        grad_wkvb,
        grad_wout,
        gain_grads[3],
        grad_gate,
        grad_upper,
        grad_down,
        statistics,
    )


def solution(mesh):
    both, row = P("row", "col"), P("row")
    swapped = P("col", "row")
    return jax.shard_map(
        per_device,
        mesh=mesh,
        in_specs=(
            both, both, row, P("row", None), row, both, row, both, both, row, both, swapped, row,
            both, both, swapped,
        ),
        out_specs=(
            both, both, row, both, row, both, both, row, both, swapped, row, both, both, swapped,
            P(),
        ),
        check_vma=False,
    )
```
